32 devices in a mesh: lat: 4 (over z), lon: 8 (over y, x, core).
Axes of the slice: x: 2, y: 2, z: 4, core: 2. Of those that a mesh axis runs over, the one named last changes fastest.
Arguments:
- spectral: bfloat16 [640, 2, 128, 640], P('lat', None, 'lon'), may hold values from -6 to 6
- wavenumber_of_slot: int32 [640], replicated, may hold values from 0 to 639, each once
- filter_strength: float32 [128], P('lon'), may hold values from 0.1 to 10
- courant: bfloat16 [2, 640, 1280, 128], P(None, 'lat', 'lon'), may hold values from -0.59765625 to 0.59765625
- sunlit_blocks: int32 [4, 8, 12], P('lat', 'lon'), may hold values from 0 to 1599, as said below
- sunlit_owner: int32 [4, 8, 12, 1], P('lat', 'lon'), may hold values from 0 to 7; in each aligned block of 12 rows (0 to 11, 12 to 23, ..., all dimensions but the last counted through in order) at most 2 rows name the same one
- radiation_in: bfloat16 [8, 128, 512], P('lon'), may hold values from -0.5 to 0.5
- radiation_mid: bfloat16 [8, 512, 512], P('lon'), may hold values from -0.25 to 0.25
- radiation_out: bfloat16 [8, 512, 128], P('lon'), may hold values from -0.25 to 0.25
Outputs:
- advected: float32 [640, 1280, 128], P('lat', 'lon')
- heating: bfloat16 [640, 1280, 128], P('lat', 'lon')
The draws below stay inside these ranges and needn't reach their ends.
Inputs may be any that keep to these rules, and one draw needn't show every extreme that they name: `wavenumber_of_slot`: each of 0 to 639 exactly once. `sunlit_blocks`: the 12 block numbers of one device are distinct. `sunlit_owner`: among the 12 blocks of one device no regime appears more than 2 times, and some device names some regime exactly 2 times.
All inputs are finite; a program needn't handle non-finite values.
Results may differ from the reference program's by a relative error of at most 0.015.
Values may be sent and summed in bfloat16 or wider, within the bound.
No kernel may reach another device: no remote copies, remote signals or barrier semaphores. Data moves between devices by JAX's collectives and lax.ppermute only.
A program may use at most 128 MiB of HBM per device.

```python
import math
import jax
import jax.numpy as jnp
import numpy as np
from jax import lax

TRUNC = 640
NLAT = 640
NLON = 1280
LEV = 128
HID = 512
BC = 16
CAP = 2
SUNLIT = 12
LATD = 160
LOND = 160
NB = 10
BLK_DEV = 1600
REGIMES = 8
N_LAT = 4
N_LON = 8


def pick_blocks(device_key):
    return jax.random.permutation(device_key, BLK_DEV)[:SUNLIT]


def draw_sunlit_blocks(key, part):
    device_keys = jax.random.split(jax.random.fold_in(key, 7), N_LAT * N_LON)
    picks = jax.vmap(pick_blocks)(device_keys)
    return picks.astype(jnp.int32).reshape(N_LAT, N_LON, SUNLIT)


def block_levels(stream_key, shape, pieces, low, high):
    def one(dim, blocks):
        draws = jax.random.uniform(jax.random.fold_in(jax.random.fold_in(stream_key, 6), dim), (blocks,), jnp.float32, low / len(pieces), high / len(pieces))
        return jnp.repeat(jnp.exp(draws), shape[dim] // blocks).reshape((-1,) + (1,) * (len(shape) - dim - 1))

    loudness = one(*pieces[0])
    for cut in pieces[1:]:
        loudness = loudness * one(*cut)
    return loudness


def deal_out(rng, own, number, rows, number_of, top, most, skew):
    ranking = jax.random.permutation(rng, number_of)
    packed, common = shares(number_of, rows * top, most, skew, True), shares(number_of, rows * top, most, skew, False)
    places = jnp.arange(number_of)

    def named(lengths, rotation):
        used = int((lengths > 0).sum())
        fixed = max(1, used // 4)
        passed = fixed + (places - fixed + rotation * (used - fixed)) % max(1, number_of - fixed)
        return jnp.zeros((number_of,), jnp.int32).at[ranking[jnp.where(places < fixed, places, passed)]].set(jnp.asarray(lengths, jnp.int32))

    lengths = jnp.where(number % 4 == 0, named(packed, number // 4), named(common, number - number // 4 - 1))
    mixed = jax.random.permutation(jax.random.fold_in(own, 3), number_of)
    donor, sink = mixed[0:number_of // 2 * 2:2], mixed[1:number_of // 2 * 2:2]
    room = jnp.minimum(lengths[donor] - 1, most - lengths[sink]) // 2
    room = jnp.where((donor == ranking[0]) | (sink == ranking[0]) | (lengths[sink] == 0), 0, jnp.maximum(room, 0))
    passed = jax.random.randint(jax.random.fold_in(own, 4), (number_of // 2,), 0, 1 << 20) % (room + 1)
    lengths = lengths.at[donor].add(-passed).at[sink].add(passed)
    items = jnp.searchsorted(jnp.cumsum(lengths), jnp.arange(rows * top), side="right").astype(jnp.int32)
    table = items.reshape(top, rows).T
    table = table[jax.random.permutation(jax.random.fold_in(own, 1), rows)]
    rotation = jax.random.randint(jax.random.fold_in(own, 2), (rows, 1), 0, top)
    return jnp.take_along_axis(table, (jnp.arange(top)[None, :] + rotation) % top, axis=1)


def shares(amount, total, bound, slope, full):
    loads = [(1 << 20) // math.isqrt(grade ** slope) + 1 for grade in range(1, amount + 1)]
    largest = bound if full else min(bound, max(-(-total // amount), total * loads[0] // sum(loads)))
    least = 1 if total - largest >= amount - 1 else 0
    counts, spare = [largest] + [least] * (amount - 1), total - largest - least * (amount - 1)
    while spare > 0:
        candidates = [i for i in range(1, amount) if counts[i] < largest] or [i for i in range(1, amount) if counts[i] < bound]
        whole, left = sum([loads[i] for i in candidates]), spare
        for i in candidates:
            more = min(bound - counts[i], max(1, left * loads[i] // whole), spare)
            counts[i] = counts[i] + more
            spare = spare - more
    return np.array(counts)


def bell_draw(stream_key, shape, spread, most, pieces=(), held_as=jnp.bfloat16):
    drawn = spread * jax.random.normal(stream_key, shape, jnp.float32)
    if pieces:
        drawn = drawn * block_levels(stream_key, shape, pieces, -0.22, 0.18)
    return jnp.clip(drawn, -most, most).astype(held_as)


def setup_inputs(seed: int = 0) -> dict:
    key_of = jax.random.split(jax.random.key(seed), 10)
    spectral = bell_draw(key_of[0], (TRUNC, 2, LEV, TRUNC), 1.0, 6.0, ((0, 4), (2, 8)))
    wavenumber_of_slot = jax.random.permutation(key_of[1], TRUNC).astype(jnp.int32)
    filter_strength = jnp.clip(jnp.exp(math.log(10.0) - 4.6051702 * jax.random.uniform(key_of[2], (LEV,), jnp.float32) ** block_levels(key_of[2], (LEV,), ((0, 8),), -0.2, 0.2)), 0.1, 10.0)
    courant = jnp.clip(jax.random.uniform(key_of[3], (2, NLAT, NLON, LEV), jnp.float32, -0.59765625, 0.59765625) * block_levels(key_of[3], (2, NLAT, NLON, LEV), ((1, 4), (2, 8)), -0.4, 0.0), -0.59765625, 0.59765625).astype(jnp.bfloat16)
    sunlit_blocks = draw_sunlit_blocks(jax.random.fold_in(key_of[9], 71), 0)
    sunlit_owner_keys = jax.random.split(jax.random.fold_in(key_of[5], 1), N_LAT * N_LON * SUNLIT // SUNLIT)
    sunlit_owner_turns = jax.random.permutation(jax.random.fold_in(key_of[5], 3), N_LAT * N_LON * SUNLIT // SUNLIT)
    sunlit_owner = jax.vmap(lambda own, number: deal_out(jax.random.fold_in(key_of[5], 2), own, number, SUNLIT, REGIMES, 1, CAP, 2))(sunlit_owner_keys, sunlit_owner_turns).reshape((N_LAT, N_LON, SUNLIT, 1))
    radiation_in = bell_draw(key_of[6], (REGIMES, LEV, HID), LEV ** -0.5, 0.5, ((0, 8),))
    radiation_mid = bell_draw(key_of[7], (REGIMES, HID, HID), HID ** -0.5, 0.25, ((0, 8),))
    radiation_out = bell_draw(key_of[8], (REGIMES, HID, LEV), HID ** -0.5, 0.25, ((0, 8),))
    return dict(spectral=spectral, wavenumber_of_slot=wavenumber_of_slot, filter_strength=filter_strength, courant=courant, sunlit_blocks=sunlit_blocks, sunlit_owner=sunlit_owner, radiation_in=radiation_in, radiation_mid=radiation_mid, radiation_out=radiation_out)


group_rows = 64

def latitude_table(degrees, latitudes):
    degree_grid = lax.broadcasted_iota(jnp.int32, (degrees, latitudes), 0)
    row_index = lax.broadcasted_iota(jnp.int32, (degrees, latitudes), 1)
    phase_count = degree_grid * (2 * row_index + 1) % (4 * latitudes)
    phase_angle = phase_count.astype(jnp.float32) * (math.pi / (2.0 * latitudes))
    return (jnp.cos(phase_angle) * math.sqrt(2.0 / degrees)).astype(jnp.bfloat16)

def longitude_table(zonal_waves, longitudes):
    total_count = zonal_waves.shape[0]
    column_index = lax.broadcasted_iota(jnp.int32, (total_count, longitudes), 1)
    phase_count = zonal_waves.astype(jnp.int32)[:, None] * column_index % longitudes
    phase_angle = phase_count.astype(jnp.float32) * (2.0 * math.pi / longitudes)
    scaling = 1.0 / math.sqrt(total_count)
    return jnp.stack([jnp.cos(phase_angle) * scaling, -jnp.sin(phase_angle) * scaling], axis=1).astype(jnp.bfloat16)

def damped(spectral, zonal_waves, strength, degrees):
    degree_grid = lax.broadcasted_iota(jnp.int32, spectral.shape, 3)
    component = lax.broadcasted_iota(jnp.int32, spectral.shape, 1)
    zonal_order = zonal_waves.astype(jnp.int32)[:, None, None, None]
    retained = (degree_grid >= zonal_order) & ((component == 0) | (zonal_order > 0))
    relative = (degree_grid * (degree_grid + 1)).astype(jnp.float32) / float(degrees * (degrees + 1))
    factor = 1.0 / (1.0 + strength[None, None, :, None] * relative * relative)
    return jnp.where(retained, spectral.astype(jnp.float32) * factor, 0.0).astype(jnp.bfloat16)

def transport(padded, zonal, meridional):
    centre = padded[1:-1, 1:-1]
    northern = padded[2:, 1:-1]
    southern = padded[:-2, 1:-1]
    eastern = padded[1:-1, 2:]
    western = padded[1:-1, :-2]
    along = centre - 0.5 * zonal * (eastern - western) + 0.5 * zonal * zonal * (eastern - 2.0 * centre + western)
    return along - 0.5 * meridional * (northern - southern) + 0.5 * meridional * meridional * (northern - 2.0 * centre + southern)

def advect(tracer, zonal, meridional):
    padded = jnp.pad(tracer, ((1, 1), (0, 0), (0, 0)))
    padded = jnp.concatenate([padded[:, -1:], padded, padded[:, :1]], axis=1)
    return transport(padded, zonal, meridional)

def regime_net(columns, w_in, w_mid, w_out):
    layer_one = jax.nn.silu(jnp.dot(columns, w_in, preferred_element_type=jnp.float32)).astype(jnp.bfloat16)
    layer_two = jax.nn.silu(jnp.dot(layer_one, w_mid, preferred_element_type=jnp.float32)).astype(jnp.bfloat16)
    return jnp.dot(layer_two, w_out, preferred_element_type=jnp.float32).astype(jnp.bfloat16)

def reference(spectral, wavenumber_of_slot, filter_strength, courant, sunlit_blocks, sunlit_owner, radiation_in, radiation_mid, radiation_out):
    filtered = damped(spectral, wavenumber_of_slot, filter_strength, TRUNC)
    coefficients = jnp.dot(filtered.reshape(-1, TRUNC), latitude_table(TRUNC, NLAT), preferred_element_type=jnp.float32)
    coefficients = coefficients.astype(jnp.bfloat16).reshape(TRUNC, 2, LEV, NLAT)
    wave_table = longitude_table(wavenumber_of_slot, NLON)
    grid_field = jnp.einsum('sclj,sck->jkl', coefficients.astype(jnp.float32), wave_table.astype(jnp.float32), precision=lax.Precision.HIGHEST).astype(jnp.bfloat16)
    zonal = courant[0].astype(jnp.float32)
    meridional = courant[1].astype(jnp.float32)
    advected = advect(advect(grid_field.astype(jnp.float32), zonal, meridional), zonal, meridional)
    state = advected.astype(jnp.bfloat16)
    sunlit = sunlit_blocks.reshape(-1).astype(jnp.int32)
    destination = sunlit_owner.reshape(-1).astype(jnp.int32)
    total_rows = sunlit.shape[0]
    device = jnp.arange(total_rows, dtype=jnp.int32) // SUNLIT
    latitude_row = device // N_LON * LATD + sunlit // NB
    first_lon = device % N_LON * LOND + sunlit % NB * BC
    lon_index = first_lon[:, None] + jnp.arange(BC, dtype=jnp.int32)[None, :]
    picked = state[latitude_row[:, None], lon_index]
    order = jnp.argsort(destination, stable=True).astype(jnp.int32)
    ranked = picked[order]
    group_sizes = lax.optimization_barrier(jnp.sum((destination[:, None] == jnp.arange(REGIMES, dtype=jnp.int32)[None, :]).astype(jnp.int32), axis=0))
    starts = (jnp.cumsum(group_sizes) - group_sizes).astype(jnp.int32)

    def regime_body(regime, result):
        w_in = radiation_in[regime]
        w_mid = radiation_mid[regime]
        w_out = radiation_out[regime]

        def block_body(sweep, total):
            offsets = jnp.arange(group_rows, dtype=jnp.int32)
            usable = sweep * group_rows + offsets < group_sizes[regime]
            take_index = jnp.minimum(starts[regime] + sweep * group_rows + offsets, total_rows - 1).astype(jnp.int32)
            columns = ranked[take_index].reshape(group_rows * BC, LEV)
            output = regime_net(columns, w_in, w_mid, w_out).astype(jnp.float32).reshape(group_rows, BC * LEV)
            output = jnp.where(usable[:, None], output, 0.0)
            return total.at[order[take_index]].add(output)
        block_total = ((group_sizes[regime] + group_rows - 1) // group_rows).astype(jnp.int32)
        return lax.fori_loop(jnp.int32(0), block_total, block_body, result)
    result = lax.fori_loop(0, REGIMES, regime_body, jnp.zeros((total_rows, BC * LEV), jnp.float32))
    heating = jnp.zeros((NLAT, NLON, LEV), jnp.float32).at[latitude_row[:, None], lon_index].set(result.reshape(total_rows, BC, LEV))
    return (advected, heating.astype(jnp.bfloat16))
```

```python
import functools
import math

import jax
import jax.numpy as jnp
import ml_dtypes
import numpy as np
from jax import lax
from jax.experimental import pallas as pl
from jax.experimental.pallas import tpu as pltpu
from jax.sharding import PartitionSpec as P

BC = 16
CAP = 2
LANES = 128
PAIR = 64
ROWS = 4
EDGE = 2
MAIN = 256
REM = LANES + 2 * LANES

F32 = jnp.float32
BF16 = jnp.bfloat16


def last_dims(lhs, rhs):
    return lax.dot_general(lhs, rhs, (((1,), (1,)), ((), ())), preferred_element_type=F32)


def latitude_rows(degrees, latitudes, bands):
    band = latitudes // bands
    first = np.arange(bands)[:, None] * band - EDGE
    rows = first + np.arange(band + 2 * EDGE)[None, :]
    phase = (np.arange(degrees)[None, None, :] * (2 * rows[:, :, None] + 1)) % (4 * latitudes)
    table = np.cos(phase * (math.pi / (2.0 * latitudes))) * math.sqrt(2.0 / degrees)
    inside = (rows >= 0) & (rows < latitudes)
    return np.where(inside[:, :, None], table, 0.0).astype(ml_dtypes.bfloat16)


def longitude_columns(waves, sources, longitudes, owners, group):
    total = waves.shape[0]
    width = longitudes // owners
    per_source = jnp.broadcast_to(
        waves.reshape(sources, total // sources, 1), (sources, total // sources, 2)
    ).reshape(sources, -1)
    rest = per_source[:, MAIN:]
    row_wave = jnp.concatenate([per_source[:, :MAIN], rest, rest], axis=1).reshape(-1)
    quarter = (jnp.arange(row_wave.shape[0], dtype=jnp.int32) % 2) * (longitudes // 4)
    first = np.arange(owners)[:, None] * width - EDGE
    main = (first + np.arange(LANES)[None, :]).reshape(owners // group, group * LANES)
    rest_columns = (first + LANES + np.arange(PAIR)[None, :]).reshape(owners // group, group * PAIR)
    columns = np.concatenate([main, rest_columns], axis=1) % longitudes
    shape = (owners // group, row_wave.shape[0], columns.shape[1])
    phase = (row_wave[None, :, None] * jnp.asarray(columns, jnp.int32)[:, None, :]) + quarter[None, :, None]
    phase = jnp.broadcast_to(phase, shape) % longitudes
    angle = phase.astype(F32) * (2.0 * math.pi / longitudes)
    return (jnp.cos(angle) * (1.0 / math.sqrt(total))).astype(BF16)


def regroup_kernel(waves_ref, x_ref, factor_ref, out_ref, scratch):
    slots, _, levels, degrees = x_ref.shape
    start = pl.program_id(0) * slots
    degree = lax.broadcasted_iota(jnp.int32, (levels, degrees), 1)
    factor = factor_ref[...]
    for s in range(slots):
        m = waves_ref[start + s]
        for c in range(2):
            least = m if c == 0 else jnp.where(m == 0, degrees, m)
            value = x_ref[s, c].astype(F32) * factor
            value = jnp.where(degree >= least, value, 0.0)
            for n in range(degrees // LANES):
                scratch[n, pl.ds((s * 2 + c) * levels, levels), :] = value[:, n * LANES : (n + 1) * LANES]
    for l in range(levels):
        for n in range(degrees // LANES):
            part = scratch[n, pl.ds(l, slots * 2, stride=levels), :]
            out_ref[l, :, n * LANES : (n + 1) * LANES] = part.astype(BF16)


def regroup(spectral, own_waves, factor):
    slots, parts, levels, degrees = spectral.shape
    block = slots // 5
    return pl.pallas_call(
        regroup_kernel,
        grid_spec=pltpu.PrefetchScalarGridSpec(
            num_scalar_prefetch=1,
            grid=(slots // block,),
            in_specs=[
                pl.BlockSpec((block, parts, levels, degrees), lambda i, w: (i, 0, 0, 0)),
                pl.BlockSpec((levels, degrees), lambda i, w: (0, 0)),
            ],
            out_specs=pl.BlockSpec((levels, block * parts, degrees), lambda i, w: (0, i, 0)),
            scratch_shapes=[pltpu.VMEM((degrees // LANES, block * parts * levels, LANES), F32)],
        ),
        out_shape=jax.ShapeDtypeStruct((levels, slots * parts, degrees), BF16),
        name="regroup",
    )(own_waves, spectral, factor)


def latitude_kernel(p_ref, b_ref, out_ref, low, high, rest):
    t = pl.program_id(0)
    half = pl.num_programs(0)
    bands = out_ref.shape[0]
    count = p_ref.shape[0]
    rows = count // bands
    table = p_ref[...]
    for h in range(2):
        result = last_dims(table, b_ref[h, 0, :MAIN, :])
        low[pl.ds(h * 8 + t, count, stride=16), :] = result[:, :LANES]
        high[pl.ds(h * 8 + t, count, stride=16), :] = result[:, LANES:]
    packed = jnp.concatenate([b_ref[0, 0, MAIN:, :], b_ref[1, 0, MAIN:, :]], axis=0)
    rest[pl.ds(t, count, stride=8), :] = last_dims(table, packed)

    @pl.when(t == half - 1)
    def _():
        for d in range(bands):
            out_ref[d, : rows * 16] = low[d * rows * 16 : (d + 1) * rows * 16].astype(BF16)
            out_ref[d, rows * 16 : rows * 32] = high[d * rows * 16 : (d + 1) * rows * 16].astype(BF16)
            out_ref[d, rows * 32 :] = rest[d * rows * 8 : (d + 1) * rows * 8].astype(BF16)


def latitude_transform(table, grouped, bands):
    count, degrees = table.shape
    levels, lanes, _ = grouped.shape
    half = levels // 2
    rows = count // bands
    split = grouped.reshape(2, half, lanes, degrees)
    return pl.pallas_call(
        latitude_kernel,
        grid=(half,),
        in_specs=[
            pl.BlockSpec((count, degrees), lambda t: (0, 0)),
            pl.BlockSpec((2, 1, lanes, degrees), lambda t: (0, t, 0, 0)),
        ],
        out_specs=pl.BlockSpec((bands, rows * 40, LANES), lambda t: (0, 0, 0)),
        out_shape=jax.ShapeDtypeStruct((bands, rows * 40, LANES), BF16),
        scratch_shapes=[
            pltpu.VMEM((count * 16, LANES), F32),
            pltpu.VMEM((count * 16, LANES), F32),
            pltpu.VMEM((count * 8, LANES), F32),
        ],
        name="latitude",
    )(table, split)


def longitude_kernel(r_ref, e_ref, out_ref, lhs):
    sources = r_ref.shape[0]
    rows = r_ref.shape[1] // 40
    group = out_ref.shape[0]

    @pl.when(pl.program_id(0) == 0)
    def _():
        lane = lax.broadcasted_iota(jnp.int32, (rows, 8, LANES), 2)
        for a in range(sources):
            at = a * REM
            lhs[:, at : at + LANES] = r_ref[a, : rows * 16]
            lhs[:, at + LANES : at + MAIN] = r_ref[a, rows * 16 : rows * 32]
            rest = r_ref[a, rows * 32 :].astype(F32).reshape(rows, 8, LANES)
            lower = jnp.where(lane < PAIR, rest, 0.0)
            upper = jnp.where(lane < PAIR, 0.0, rest)
            both = jnp.concatenate([lower, upper], axis=1).reshape(rows * 16, LANES)
            lhs[:, at + MAIN : at + REM] = both.astype(BF16)

    result = jnp.dot(lhs[...], e_ref[0], preferred_element_type=F32)
    for i in range(group):
        out_ref[i, : rows * 16] = result[:, i * LANES : (i + 1) * LANES].astype(BF16)
    lane = lax.broadcasted_iota(jnp.int32, (rows * 8, LANES), 1)
    for i in range(group // 2):
        at = group * LANES + i * LANES
        pairs = result[:, at : at + LANES].reshape(rows // 2, 2, 16, LANES)
        even = pairs[:, 0].reshape(rows * 8, LANES)
        odd = pairs[:, 1].reshape(rows * 8, LANES)
        turned_even = pltpu.roll(even, PAIR, 1)
        turned_odd = pltpu.roll(odd, PAIR, 1)
        out_ref[2 * i, rows * 16 :] = jnp.where(lane < PAIR, even, turned_odd).astype(BF16)
        out_ref[2 * i + 1, rows * 16 :] = jnp.where(lane < PAIR, turned_even, odd).astype(BF16)


def longitude_transform(received, table, owners):
    sources, length, _ = received.shape
    rows = length // 40
    parts, depth, width = table.shape
    group = owners // parts
    return pl.pallas_call(
        longitude_kernel,
        grid=(parts,),
        in_specs=[
            pl.BlockSpec((sources, length, LANES), lambda t: (0, 0, 0)),
            pl.BlockSpec((1, depth, width), lambda t: (t, 0, 0)),
        ],
        out_specs=pl.BlockSpec((group, rows * 24, LANES), lambda t: (t, 0, 0)),
        out_shape=jax.ShapeDtypeStruct((owners, rows * 24, LANES), BF16),
        scratch_shapes=[pltpu.VMEM((rows * 16, depth), BF16)],
        name="longitude",
    )(received, table)


def moved(centre, east, west, north, south, u, v):
    twice = 2.0 * centre
    along = (0.5 * u) * (u * ((east + west) - twice) - (east - west))
    across = (0.5 * v) * (v * ((north + south) - twice) - (north - south))
    return centre + (along + across)


def transport_kernel(first, *refs):
    if first:
        main_ref, rest_ref, uv_ref, out_ref, q, uv, s = refs
    else:
        main_ref, rest_ref, uv_ref, old_main, old_rest, _, out_ref, q, uv, s = refs
    t = pl.program_id(0)
    base = (t % 2) * ROWS
    prior = ROWS - base
    out_cols = out_ref.shape[1]
    wide = uv_ref.shape[2]
    eye_row = lax.broadcasted_iota(jnp.int32, (LANES, LANES), 0)
    eye_col = lax.broadcasted_iota(jnp.int32, (LANES, LANES), 1)
    eye = jnp.where(eye_row == eye_col, 1.0, 0.0).astype(BF16)

    def unpack(main, rest):
        for r in range(ROWS // 2):
            for j in (2 * r, 2 * r + 1):
                tile = main[:, j * 16 : (j + 1) * 16, :].reshape(LANES, LANES)
                q[base + j, :LANES, :] = last_dims(eye, tile)
            tile = rest[:, r * 16 : (r + 1) * 16, :].reshape(LANES, LANES)
            turned = last_dims(eye, tile)
            q[base + 2 * r, LANES : LANES + PAIR, :] = turned[:PAIR]
            q[base + 2 * r + 1, LANES : LANES + PAIR, :] = turned[PAIR:]

    if first:
        unpack(main_ref, rest_ref)
    else:

        @pl.when(t == 0)
        def _():
            unpack(old_main, old_rest)

        @pl.when(t > 0)
        def _():
            unpack(main_ref, rest_ref)

    for i in range(ROWS):
        for k in range(2):
            uv[k, base + i] = uv_ref[k, i].astype(F32)

    def at(i):
        return base + i if i >= 0 else prior + ROWS + i

    step = 24
    for i in range(-1, ROWS - 1):
        for o in range(0, wide, step):
            s[at(i), pl.ds(o, step), :] = moved(
                q[at(i), pl.ds(o + 1, step), :],
                q[at(i), pl.ds(o + 2, step), :],
                q[at(i), pl.ds(o, step), :],
                q[at(i + 1), pl.ds(o + 1, step), :],
                q[at(i - 1), pl.ds(o + 1, step), :],
                uv[0, at(i), pl.ds(o, step), :],
                uv[1, at(i), pl.ds(o, step), :],
            )
    step = 32
    for i in range(-2, ROWS - 2):
        for o in range(0, out_cols, step):
            out_ref[i + 2, pl.ds(o, step), :] = moved(
                s[at(i), pl.ds(o + 1, step), :],
                s[at(i), pl.ds(o + 2, step), :],
                s[at(i), pl.ds(o, step), :],
                s[at(i + 1), pl.ds(o + 1, step), :],
                s[at(i - 1), pl.ds(o + 1, step), :],
                uv[0, at(i), pl.ds(o + 1, step), :],
                uv[1, at(i), pl.ds(o + 1, step), :],
            )


def transport(fields, index, starts, courant, advected, shape):
    field = fields[index]
    owners, length, _ = field.shape
    rows = length // 24
    blocks = rows // ROWS
    offset = starts[index] // ROWS
    first = index == 0
    wide = courant.shape[2]
    lead = 0 if first else 1
    main = (owners, ROWS * 16, LANES)
    rest = (owners, ROWS * 8, LANES)

    def rest_at(count):
        return count * ROWS * 16 // (ROWS * 8)

    in_specs = [
        pl.BlockSpec(main, lambda t: (0, jnp.maximum(t - lead, 0), 0)),
        pl.BlockSpec(rest, lambda t: (0, rest_at(blocks) + jnp.maximum(t - lead, 0), 0)),
        pl.BlockSpec((2, ROWS, wide, LANES), lambda t: (0, offset + t - lead, 0, 0)),
    ]
    operands = [field, field, courant]
    aliases = {}
    if not first:
        old = fields[index - 1]
        old_blocks = old.shape[1] // 24 // ROWS
        in_specs += [
            pl.BlockSpec(main, lambda t: (0, old_blocks - 1, 0)),
            pl.BlockSpec(rest, lambda t: (0, rest_at(old_blocks) + old_blocks - 1, 0)),
            pl.BlockSpec(memory_space=pl.ANY),
        ]
        operands += [old, old, advected]
        aliases = {5: 0}
    return pl.pallas_call(
        functools.partial(transport_kernel, first),
        grid=(blocks + lead,),
        in_specs=in_specs,
        out_specs=pl.BlockSpec(
            (ROWS,) + shape[1:], lambda t: (jnp.maximum(t, 1) - 1 + offset - lead, 0, 0)
        ),
        out_shape=jax.ShapeDtypeStruct(shape, F32),
        scratch_shapes=[
            pltpu.VMEM((2 * ROWS, LANES + PAIR, LANES), F32),
            pltpu.VMEM((2, 2 * ROWS, wide, LANES), F32),
            pltpu.VMEM((2 * ROWS, wide, LANES), F32),
        ],
        input_output_aliases=aliases,
        name="transport",
    )(*operands)


def gather_kernel(blocks_ref, places_ref, state_ref, out_ref):
    t = pl.program_id(0)

    @pl.when(t == 0)
    def _():
        out_ref[...] = jnp.zeros_like(out_ref)

    at = pl.multiple_of(places_ref[t] * BC, BC)
    out_ref[pl.ds(at, BC), :] = state_ref[0].astype(BF16)


def gather_blocks(advected, blocks, places, owners):
    lon_cols, levels = advected.shape[1:]
    across = lon_cols // BC
    return pl.pallas_call(
        gather_kernel,
        grid_spec=pltpu.PrefetchScalarGridSpec(
            num_scalar_prefetch=2,
            grid=(blocks.shape[0],),
            in_specs=[
                pl.BlockSpec((1, BC, levels), lambda t, b, p: (b[t] // across, b[t] % across, 0))
            ],
            out_specs=pl.BlockSpec((owners * CAP * BC, levels), lambda t, b, p: (0, 0)),
        ),
        out_shape=jax.ShapeDtypeStruct((owners * CAP * BC, levels), BF16),
        name="gather_blocks",
    )(blocks, places, advected)


def network_kernel(x_ref, in_ref, mid_ref, out_ref, y_ref):
    def silu(v):
        return (v / (1.0 + jnp.exp(-v))).astype(BF16)

    one = silu(jnp.dot(x_ref[...], in_ref[...], preferred_element_type=F32))
    two = silu(jnp.dot(one, mid_ref[...], preferred_element_type=F32))
    y_ref[...] = jnp.dot(two, out_ref[...], preferred_element_type=F32).astype(BF16)


def network(columns, w_in, w_mid, w_out):
    return pl.pallas_call(
        network_kernel,
        out_shape=jax.ShapeDtypeStruct((columns.shape[0], w_out.shape[1]), BF16),
        name="network",
    )(columns, w_in, w_mid, w_out)


def scatter_kernel(blocks_ref, places_ref, rows_ref, _, out_ref):
    at = pl.multiple_of(places_ref[pl.program_id(0)] * BC, BC)
    out_ref[0] = rows_ref[pl.ds(at, BC), :]


def scatter_blocks(rows, blocks, places, empty):
    levels = empty.shape[2]
    across = empty.shape[1] // BC
    return pl.pallas_call(
        scatter_kernel,
        grid_spec=pltpu.PrefetchScalarGridSpec(
            num_scalar_prefetch=2,
            grid=(blocks.shape[0],),
            in_specs=[
                pl.BlockSpec(rows.shape, lambda t, b, p: (0, 0)),
                pl.BlockSpec(memory_space=pl.ANY),
            ],
            out_specs=pl.BlockSpec(
                (1, BC, levels), lambda t, b, p: (b[t] // across, b[t] % across, 0)
            ),
        ),
        out_shape=jax.ShapeDtypeStruct(empty.shape, BF16),
        input_output_aliases={3: 0},
        name="scatter_blocks",
    )(blocks, places, rows, empty)


def widened_courant(courant):
    bands = lax.axis_size("lat")
    owners = lax.axis_size("lon")
    up = [(i, i + 1) for i in range(bands - 1)]
    down = [(i + 1, i) for i in range(bands - 1)]
    south = lax.ppermute(courant[:, -1:], "lat", up)
    north = lax.ppermute(courant[:, :1], "lat", down)
    tall = jnp.concatenate([south, courant, north], axis=1)
    ahead = [(i, (i + 1) % owners) for i in range(owners)]
    back = [(j, i) for i, j in ahead]
    west = lax.ppermute(tall[:, :, -1:], "lon", ahead)
    east = lax.ppermute(tall[:, :, :1], "lon", back)
    wide = jnp.concatenate([west, tall, east], axis=2)
    spare = -wide.shape[2] % 24
    return jnp.pad(wide, ((0, 0), (1, 1), (0, spare), (0, 0)))


def chunk_sizes(rows):
    blocks = rows // ROWS
    cuts = [round(blocks * f) for f in (0.0, 0.3, 0.58, 0.82)] + [blocks]
    return [(b - a) * ROWS for a, b in zip(cuts, cuts[1:])]


def tiled_body(
    spectral,
    wavenumber_of_slot,
    filter_strength,
    courant,
    sunlit_blocks,
    sunlit_owner,
    radiation_in,
    radiation_mid,
    radiation_out,
):
    bands = lax.axis_size("lat")
    owners = lax.axis_size("lon")
    slots, parts, own_levels, degrees = spectral.shape
    _, lat_rows, lon_cols, levels = courant.shape
    latitudes = lat_rows * bands
    longitudes = lon_cols * owners
    own_waves = lax.dynamic_slice_in_dim(wavenumber_of_slot, lax.axis_index("lat") * slots, slots)
    degree = jnp.arange(degrees, dtype=jnp.int32)
    relative = (degree * (degree + 1)).astype(F32) / float(degrees * (degrees + 1))
    factor = 1.0 / (1.0 + filter_strength[:, None] * relative[None, :] * relative[None, :])

    rows = lat_rows + 2 * EDGE
    sizes = chunk_sizes(rows)
    starts = [sum(sizes[:i]) for i in range(len(sizes))]
    lat_table = latitude_rows(degrees, latitudes, bands)
    grouped = regroup(spectral, own_waves, factor)
    received = []
    for start, size in zip(starts, sizes):
        piece = jnp.asarray(lat_table[:, start : start + size].reshape(bands * size, degrees))
        sent = latitude_transform(piece, grouped, bands)
        received.append(lax.all_to_all(sent, "lat", split_axis=0, concat_axis=0, tiled=True))

    lon_table = longitude_columns(wavenumber_of_slot, bands, longitudes, owners, owners // 2)
    wide = widened_courant(courant)
    fields = []
    for piece in received:
        sent = longitude_transform(piece, lon_table, owners)
        fields.append(lax.all_to_all(sent, "lon", split_axis=0, concat_axis=0, tiled=True))

    advected = None
    for index in range(len(fields)):
        advected = transport(fields, index, starts, wide, advected, (lat_rows, lon_cols, levels))

    blocks = sunlit_blocks.reshape(-1)
    regime = sunlit_owner.reshape(-1)
    listed = blocks.shape[0]
    order = jnp.arange(listed, dtype=jnp.int32)
    same = (regime[:, None] == regime[None, :]) & (order[None, :] < order[:, None])
    places = regime * CAP + jnp.sum(same.astype(jnp.int32), axis=1)
    picked = gather_blocks(advected, blocks, places, owners).reshape(owners, CAP * BC, levels)
    arrived = lax.all_to_all(picked, "lon", split_axis=0, concat_axis=0, tiled=True)
    computed = network(
        arrived.reshape(owners * CAP * BC, levels),
        radiation_in[0],
        radiation_mid[0],
        radiation_out[0],
    ).reshape(owners, CAP * BC, levels)
    returned = lax.all_to_all(computed, "lon", split_axis=0, concat_axis=0, tiled=True)
    empty = jnp.zeros((lat_rows, lon_cols, levels), BF16)
    heating = scatter_blocks(
        returned.reshape(owners * CAP * BC, levels), blocks, places, empty
    )
    return (advected, heating)


def with_halo(array, sides, width):
    for axis, dim in sides:
        count, length = (lax.axis_size(axis), array.shape[dim])
        up = [(i, (i + 1) % count) for i in range(count)]
        down = [(j, i) for i, j in up]
        last = lax.slice_in_dim(array, length - width, length, axis=dim)
        leading = lax.slice_in_dim(array, 0, width, axis=dim)
        before = lax.ppermute(last, axis, up)
        after = lax.ppermute(leading, axis, down)
        array = jnp.concatenate([before, array, after], axis=dim)
    return array


def latitude_table(degrees, latitudes):
    degree_grid = lax.broadcasted_iota(jnp.int32, (degrees, latitudes), 0)
    row_index = lax.broadcasted_iota(jnp.int32, (degrees, latitudes), 1)
    phase_count = degree_grid * (2 * row_index + 1) % (4 * latitudes)
    phase_angle = phase_count.astype(jnp.float32) * (math.pi / (2.0 * latitudes))
    return (jnp.cos(phase_angle) * math.sqrt(2.0 / degrees)).astype(jnp.bfloat16)


def longitude_table(zonal_waves, longitudes):
    total_count = zonal_waves.shape[0]
    column_index = lax.broadcasted_iota(jnp.int32, (total_count, longitudes), 1)
    phase_count = zonal_waves[:, None] * column_index % longitudes
    phase_angle = phase_count.astype(jnp.float32) * (2.0 * math.pi / longitudes)
    scaling = 1.0 / math.sqrt(total_count)
    return jnp.stack(
        [jnp.cos(phase_angle) * scaling, -jnp.sin(phase_angle) * scaling], axis=1
    ).astype(jnp.bfloat16)


def damped(spectral, zonal_waves, strength, degrees):
    degree_grid = lax.broadcasted_iota(jnp.int32, spectral.shape, 3)
    component = lax.broadcasted_iota(jnp.int32, spectral.shape, 1)
    zonal_order = zonal_waves[:, None, None, None]
    retained = (degree_grid >= zonal_order) & ((component == 0) | (zonal_order > 0))
    relative = (degree_grid * (degree_grid + 1)).astype(jnp.float32) / float(
        degrees * (degrees + 1)
    )
    factor = 1.0 / (1.0 + strength[None, None, :, None] * relative * relative)
    return jnp.where(retained, spectral.astype(jnp.float32) * factor, 0.0).astype(jnp.bfloat16)


def plain_transport(padded, zonal, meridional):
    centre = padded[1:-1, 1:-1]
    northern = padded[2:, 1:-1]
    southern = padded[:-2, 1:-1]
    eastern = padded[1:-1, 2:]
    western = padded[1:-1, :-2]
    along = (
        centre
        - 0.5 * zonal * (eastern - western)
        + 0.5 * zonal * zonal * (eastern - 2.0 * centre + western)
    )
    return (
        along
        - 0.5 * meridional * (northern - southern)
        + 0.5 * meridional * meridional * (northern - 2.0 * centre + southern)
    )


def clear_poles(padded, depth, lat_dim):
    position = lax.axis_index("lat")
    extent = padded.shape[lat_dim]
    lat_index = lax.broadcasted_iota(jnp.int32, padded.shape, lat_dim)
    lower_rim = (position == 0) & (lat_index < depth)
    upper_rim = (position == lax.axis_size("lat") - 1) & (lat_index >= extent - depth)
    return jnp.where(lower_rim | upper_rim, jnp.zeros_like(padded), padded)


def regime_net(columns, w_in, w_mid, w_out):
    layer_one = jax.nn.silu(
        jnp.einsum("abcl,lh->abch", columns, w_in, preferred_element_type=jnp.float32)
    ).astype(jnp.bfloat16)
    layer_two = jax.nn.silu(
        jnp.einsum("abch,hg->abcg", layer_one, w_mid, preferred_element_type=jnp.float32)
    ).astype(jnp.bfloat16)
    return jnp.einsum("abcg,gl->abcl", layer_two, w_out, preferred_element_type=jnp.float32).astype(
        jnp.bfloat16
    )


def plain_body(
    spectral,
    wavenumber_of_slot,
    filter_strength,
    courant,
    sunlit_blocks,
    sunlit_owner,
    radiation_in,
    radiation_mid,
    radiation_out,
):
    own_count = spectral.shape[0]
    degrees = spectral.shape[3]
    own_waves = lax.dynamic_slice_in_dim(
        wavenumber_of_slot, lax.axis_index("lat") * own_count, own_count
    )
    filtered = damped(spectral, own_waves, filter_strength, degrees)
    coefficients = jnp.einsum(
        "scln,nj->sclj", filtered, latitude_table(degrees, courant.shape[1] * lax.axis_size("lat")), preferred_element_type=jnp.float32
    ).astype(jnp.bfloat16)
    wave_table = longitude_table(wavenumber_of_slot, courant.shape[2] * lax.axis_size("lon"))
    level_slab = jnp.einsum(
        "sclj,sck->jkl",
        lax.all_to_all(coefficients, "lat", split_axis=3, concat_axis=0, tiled=True),
        wave_table,
        preferred_element_type=jnp.float32,
    ).astype(jnp.bfloat16)
    grid_field = lax.all_to_all(level_slab, "lon", split_axis=1, concat_axis=2, tiled=True)
    zonal = courant[0].astype(jnp.float32)
    meridional = courant[1].astype(jnp.float32)
    stacked = jnp.concatenate([grid_field[None], courant], axis=0)
    widened = clear_poles(with_halo(stacked, (("lat", 1), ("lon", 2)), 2), 2, 1)
    tracer = widened[0].astype(jnp.float32)
    wide_zonal = widened[1].astype(jnp.float32)
    wide_meridional = widened[2].astype(jnp.float32)
    tracer = plain_transport(tracer, wide_zonal[1:-1, 1:-1], wide_meridional[1:-1, 1:-1])
    advected = plain_transport(tracer, zonal, meridional)
    state = advected.astype(jnp.bfloat16)
    lat_rows, lon_cols, levels = state.shape
    owners = lax.axis_size("lon")
    blocks = state.reshape(lat_rows * (lon_cols // BC), BC * levels)
    sunlit = sunlit_blocks.reshape(-1)
    destination = sunlit_owner.reshape(-1)
    listed = sunlit.shape[0]
    picked = jnp.take(blocks, sunlit, axis=0)
    position_of = destination * listed + lax.iota(jnp.int32, listed)
    select = (
        position_of[:, None] == lax.broadcasted_iota(jnp.int32, (listed, owners * listed), 1)
    ).astype(jnp.bfloat16)
    outgoing = jnp.einsum("sp,sd->pd", select, picked, preferred_element_type=jnp.float32).astype(
        jnp.bfloat16
    )
    outgoing = outgoing.reshape(owners, listed, BC, levels)
    computed = regime_net(
        lax.all_to_all(outgoing, "lon", split_axis=0, concat_axis=0, tiled=True),
        radiation_in[0],
        radiation_mid[0],
        radiation_out[0],
    )
    returned = lax.all_to_all(computed, "lon", split_axis=0, concat_axis=0, tiled=True).reshape(
        owners * listed, BC * levels
    )
    own_rows = jnp.einsum("sp,pd->sd", select, returned, preferred_element_type=jnp.float32).astype(
        jnp.bfloat16
    )
    covering = (
        sunlit[:, None] == lax.broadcasted_iota(jnp.int32, (listed, blocks.shape[0]), 1)
    ).astype(jnp.bfloat16)
    heating = jnp.einsum(
        "sb,sd->bd", covering, own_rows, preferred_element_type=jnp.float32
    ).astype(jnp.bfloat16)
    return (advected, heating.reshape(lat_rows, lon_cols, levels))


def fits(spectral, courant, bands, owners):
    total, parts, levels, degrees = spectral.shape
    width = courant.shape[2] // owners
    height = courant.shape[1] // bands
    return (
        parts == 2
        and levels == LANES
        and levels // owners == 16
        and 2 * (total // bands) == MAIN + PAIR
        and degrees % LANES == 0
        and (total // bands) % 5 == 0
        and height % ROWS == 0
        and width % 32 == 0
        and LANES < width + 2 * EDGE <= LANES + PAIR - 8
    )


def solution(mesh):
    in_specs = (
        P("lat", None, "lon", None),
        P(),
        P("lon"),
        P(None, "lat", "lon", None),
        P("lat", "lon", None),
        P("lat", "lon", None, None),
        P("lon", None, None),
        P("lon", None, None),
        P("lon", None, None),
    )
    out_specs = (P("lat", "lon", None), P("lat", "lon", None))
    bands, owners = mesh.shape["lat"], mesh.shape["lon"]

    def run(*arrays):
        body = tiled_body if fits(arrays[0], arrays[3], bands, owners) else plain_body
        return jax.shard_map(
            body, mesh=mesh, in_specs=in_specs, out_specs=out_specs, check_vma=False
        )(*arrays)

    return run
```

```python
import functools
import math

import jax
import jax.numpy as jnp
import ml_dtypes
import numpy as np
from jax import lax
from jax.experimental import pallas as pl
from jax.experimental.pallas import tpu as pltpu
from jax.sharding import PartitionSpec as P

BC = 16
LANES = 128
PAIR = 64
ROWS = 4
EDGE = 2
MAIN = 256
REM = LANES + 2 * LANES


F32 = jnp.float32
BF16 = jnp.bfloat16


def last_dims(lhs, rhs):
    return lax.dot_general(lhs, rhs, (((1,), (1,)), ((), ())), preferred_element_type=F32)


def latitude_rows(degrees, latitudes, bands):
    band = latitudes // bands
    first = np.arange(bands)[:, None] * band - EDGE
    rows = first + np.arange(band + 2 * EDGE)[None, :]
    phase = (np.arange(degrees)[None, None, :] * (2 * rows[:, :, None] + 1)) % (4 * latitudes)
    table = np.cos(phase * (math.pi / (2.0 * latitudes))) * math.sqrt(2.0 / degrees)
    inside = (rows >= 0) & (rows < latitudes)
    return np.where(inside[:, :, None], table, 0.0).astype(ml_dtypes.bfloat16)


def turn(count, period):
    quarter = period / 4.0
    turns = jnp.floor(count * (1.0 / quarter) + 0.5)
    x = (count - turns * quarter) * (2.0 * math.pi / period)
    y = x * x
    cos = 1.0 + y * (-1.0 / 2 + y * (1.0 / 24 + y * (-1.0 / 720 + y * (1.0 / 40320))))
    sin = x * (1.0 + y * (-1.0 / 6 + y * (1.0 / 120 + y * (-1.0 / 5040 + y * (1.0 / 362880)))))
    quadrant = turns.astype(jnp.int32) & 3
    odd = (quadrant & 1) == 1
    cos_part = jnp.where(odd, sin, cos)
    sin_part = jnp.where(odd, cos, sin)
    cos_minus = (quadrant == 1) | (quadrant == 2)
    sin_minus = quadrant >= 2
    return jnp.where(cos_minus, -cos_part, cos_part), jnp.where(sin_minus, -sin_part, sin_part)


def longitude_table_kernel(width, period, scale, wave_ref, main_ref, rest_ref):
    owners = main_ref.shape[0]
    depth = wave_ref.shape[0]
    wave = wave_ref[...]
    shape = (depth, 2 * LANES)
    lane = lax.broadcasted_iota(jnp.int32, shape, 1)
    row = lax.broadcasted_iota(jnp.int32, shape, 0)
    column = jnp.where(lane < LANES + PAIR, lane, lane - PAIR) - EDGE
    count = wave * column + (row & 1) * (period // 4)
    cos, sin = turn(count.astype(F32), period)
    cos = cos * scale
    sin = sin * scale
    owner = lax.broadcasted_iota(jnp.int32, (depth, LANES), 1) & (owners - 1)
    shift_cos, shift_sin = turn((wave * owner * width).astype(F32), period)
    for q in range(owners):
        value = cos[:, :LANES] * shift_cos[:, q : q + 1] - sin[:, :LANES] * shift_sin[:, q : q + 1]
        main_ref[q] = value.astype(BF16)
    low = lax.broadcasted_iota(jnp.int32, (depth, LANES), 1) < PAIR
    for t in range(owners // 2):
        q = 2 * t
        pair_cos = jnp.where(low, shift_cos[:, q : q + 1], shift_cos[:, q + 1 : q + 2])
        pair_sin = jnp.where(low, shift_sin[:, q : q + 1], shift_sin[:, q + 1 : q + 2])
        rest_ref[t] = (cos[:, LANES:] * pair_cos - sin[:, LANES:] * pair_sin).astype(BF16)


def longitude_columns(waves, sources, longitudes, owners):
    total = waves.shape[0]
    per_source = jnp.broadcast_to(
        waves.reshape(sources, total // sources, 1), (sources, total // sources, 2)
    ).reshape(sources, -1)
    rest = per_source[:, MAIN:]
    row_wave = jnp.concatenate([per_source[:, :MAIN], rest, rest], axis=1).reshape(-1, 1)
    kernel = functools.partial(
        longitude_table_kernel, longitudes // owners, longitudes, 1.0 / math.sqrt(total)
    )
    return pl.pallas_call(
        kernel,
        grid=(sources,),
        in_specs=[pl.BlockSpec((REM, 1), lambda a: (a, 0))],
        out_specs=[
            pl.BlockSpec((owners, REM, LANES), lambda a: (0, a, 0)),
            pl.BlockSpec((owners // 2, REM, LANES), lambda a: (0, a, 0)),
        ],
        out_shape=[
            jax.ShapeDtypeStruct((owners, sources * REM, LANES), BF16),
            jax.ShapeDtypeStruct((owners // 2, sources * REM, LANES), BF16),
        ],
        name="longitude_table",
    )(row_wave)


def regroup_kernel(waves_ref, x_ref, factor_ref, out_ref, scratch):
    slots, _, levels, degrees = x_ref.shape
    start = pl.program_id(0) * slots
    degree = lax.broadcasted_iota(jnp.int32, (levels, degrees), 1)
    factor = factor_ref[...]
    for s in range(slots):
        m = waves_ref[start + s]
        for c in range(2):
            least = m if c == 0 else jnp.where(m == 0, degrees, m)
            value = x_ref[s, c].astype(F32) * factor
            value = jnp.where(degree >= least, value, 0.0)
            for n in range(degrees // LANES):
                scratch[n, pl.ds((s * 2 + c) * levels, levels), :] = value[:, n * LANES : (n + 1) * LANES]
    for l in range(levels):
        for n in range(degrees // LANES):
            part = scratch[n, pl.ds(l, slots * 2, stride=levels), :]
            out_ref[l, :, n * LANES : (n + 1) * LANES] = part.astype(BF16)


def regroup(spectral, own_waves, factor):
    slots, parts, levels, degrees = spectral.shape
    block = slots // 5
    return pl.pallas_call(
        regroup_kernel,
        grid_spec=pltpu.PrefetchScalarGridSpec(
            num_scalar_prefetch=1,
            grid=(slots // block,),
            in_specs=[
                pl.BlockSpec((block, parts, levels, degrees), lambda i, w: (i, 0, 0, 0)),
                pl.BlockSpec((levels, degrees), lambda i, w: (0, 0)),
            ],
            out_specs=pl.BlockSpec((levels, block * parts, degrees), lambda i, w: (0, i, 0)),
            scratch_shapes=[pltpu.VMEM((degrees // LANES, block * parts * levels, LANES), F32)],
        ),
        out_shape=jax.ShapeDtypeStruct((levels, slots * parts, degrees), BF16),
        name="regroup",
    )(own_waves, spectral, factor)


def latitude_kernel(place_ref, p_ref, b_ref, *refs):
    outs, (low, high, rest) = refs[:-3], refs[-3:]
    t = pl.program_id(0)
    half = pl.num_programs(0)
    bands = len(outs)
    count = p_ref.shape[0]
    rows = count // bands
    table = p_ref[...]
    for h in range(2):
        result = last_dims(table, b_ref[h, 0, :MAIN, :])
        low[pl.ds(h * 8 + t, count, stride=16), :] = result[:, :LANES]
        high[pl.ds(h * 8 + t, count, stride=16), :] = result[:, LANES:]
    packed = jnp.concatenate([b_ref[0, 0, MAIN:, :], b_ref[1, 0, MAIN:, :]], axis=0)
    rest[pl.ds(t, count, stride=8), :] = last_dims(table, packed)

    @pl.when(t == half - 1)
    def _():
        for shift, out in enumerate(outs):
            band = (place_ref[0] + shift) % bands
            at = pl.multiple_of(band * (rows * 16), 16)
            out[: rows * 16] = low[pl.ds(at, rows * 16), :].astype(BF16)
            out[rows * 16 : rows * 32] = high[pl.ds(at, rows * 16), :].astype(BF16)
            at = pl.multiple_of(band * (rows * 8), 8)
            out[rows * 32 :] = rest[pl.ds(at, rows * 8), :].astype(BF16)


def latitude_transform(table, grouped, place, bands):
    count, degrees = table.shape
    levels, lanes, _ = grouped.shape
    half = levels // 2
    rows = count // bands
    split = grouped.reshape(2, half, lanes, degrees)
    return pl.pallas_call(
        latitude_kernel,
        grid_spec=pltpu.PrefetchScalarGridSpec(
            num_scalar_prefetch=1,
            grid=(half,),
            in_specs=[
                pl.BlockSpec((count, degrees), lambda t, p: (0, 0)),
                pl.BlockSpec((2, 1, lanes, degrees), lambda t, p: (0, t, 0, 0)),
            ],
            out_specs=[pl.BlockSpec((rows * 40, LANES), lambda t, p: (0, 0))] * bands,
            scratch_shapes=[
                pltpu.VMEM((count * 16, LANES), F32),
                pltpu.VMEM((count * 16, LANES), F32),
                pltpu.VMEM((count * 8, LANES), F32),
            ],
        ),
        out_shape=[jax.ShapeDtypeStruct((rows * 40, LANES), BF16)] * bands,
        name="latitude",
    )(place, table, split)


def longitude_kernel(place_ref, *refs):
    pieces, (main_ref, rest_ref, out_ref, lhs) = refs[:-4], refs[-4:]
    sources = len(pieces)
    rows = pieces[0].shape[0] // 40
    group = out_ref.shape[0]

    @pl.when(pl.program_id(0) == 0)
    def _():
        lane = lax.broadcasted_iota(jnp.int32, (rows, 8, LANES), 2)
        for shift, piece in enumerate(pieces):
            a = (place_ref[0] + sources - shift) % sources
            lhs[a, :, :LANES] = piece[: rows * 16]
            lhs[a, :, LANES:MAIN] = piece[rows * 16 : rows * 32]
            rest = piece[rows * 32 :].astype(F32).reshape(rows, 8, LANES)
            lower = jnp.where(lane < PAIR, rest, 0.0)
            upper = jnp.where(lane < PAIR, 0.0, rest)
            both = jnp.concatenate([lower, upper], axis=1).reshape(rows * 16, LANES)
            lhs[a, :, MAIN:] = both.astype(BF16)

    left = jnp.concatenate([lhs[a] for a in range(sources)], axis=1)

    def columns(ref, i):
        right = jnp.concatenate([ref[i], ref[i + 1]], axis=1)
        return jnp.dot(left, right, preferred_element_type=F32)

    for i in range(0, group, 2):
        result = columns(main_ref, i).astype(BF16)
        out_ref[i, : rows * 16] = result[:, :LANES]
        out_ref[i + 1, : rows * 16] = result[:, LANES:]
    lane = lax.broadcasted_iota(jnp.int32, (rows * 8, LANES), 1)
    for i in range(0, group // 2, 2):
        result = columns(rest_ref, i)
        for h in range(2):
            pairs = result[:, h * LANES : (h + 1) * LANES].reshape(rows // 2, 2, 16, LANES)
            even = pairs[:, 0].reshape(rows * 8, LANES)
            odd = pairs[:, 1].reshape(rows * 8, LANES)
            turned_even = pltpu.roll(even, PAIR, 1)
            turned_odd = pltpu.roll(odd, PAIR, 1)
            q = 2 * (i + h)
            out_ref[q, rows * 16 :] = jnp.where(lane < PAIR, even, turned_odd).astype(BF16)
            out_ref[q + 1, rows * 16 :] = jnp.where(lane < PAIR, turned_even, odd).astype(BF16)


def longitude_transform(pieces, tables, place):
    main, rest = tables
    sources = len(pieces)
    length = pieces[0].shape[0]
    rows = length // 40
    owners, depth, _ = main.shape
    group = owners // 2
    return pl.pallas_call(
        longitude_kernel,
        grid_spec=pltpu.PrefetchScalarGridSpec(
            num_scalar_prefetch=1,
            grid=(owners // group,),
            in_specs=[pl.BlockSpec((length, LANES), lambda t, p: (0, 0))] * sources
            + [
                pl.BlockSpec((group, depth, LANES), lambda t, p: (t, 0, 0)),
                pl.BlockSpec((group // 2, depth, LANES), lambda t, p: (t, 0, 0)),
            ],
            out_specs=pl.BlockSpec((group, rows * 24, LANES), lambda t, p: (t, 0, 0)),
            scratch_shapes=[pltpu.VMEM((sources, rows * 16, REM), BF16)],
        ),
        out_shape=jax.ShapeDtypeStruct((owners, rows * 24, LANES), BF16),
        name="longitude",
    )(place, *pieces, main, rest)


def moved(centre, east, west, north, south, u, v):
    twice = 2.0 * centre
    along = (0.5 * u) * (u * ((east + west) - twice) - (east - west))
    across = (0.5 * v) * (v * ((north + south) - twice) - (north - south))
    return centre + (along + across)


INNER = 8


def transport_kernel(first, last, offset, *refs):
    main_ref, rest_ref, lower_ref, upper_ref, edge_ref, south_ref, north_ref = refs[:7]
    if first:
        out_ref, q, uv, s = refs[7:]
    else:
        old_main, old_rest, _, out_ref, q, uv, s = refs[7:]
    t = pl.program_id(0)
    block = t + offset
    base = (t % 2) * ROWS
    prior = ROWS - base
    cols = out_ref.shape[1]
    edge_rows = edge_ref.shape[1]
    eye_row = lax.broadcasted_iota(jnp.int32, (LANES, LANES), 0)
    eye_col = lax.broadcasted_iota(jnp.int32, (LANES, LANES), 1)
    eye = jnp.where(eye_row == eye_col, 1.0, 0.0).astype(BF16)

    def unpack(main, rest):
        for r in range(ROWS // 2):
            for j in (2 * r, 2 * r + 1):
                tile = main[:, j * 16 : (j + 1) * 16, :].reshape(LANES, LANES)
                q[base + j, :LANES, :] = last_dims(eye, tile)
            tile = rest[:, r * 16 : (r + 1) * 16, :].reshape(LANES, LANES)
            turned = last_dims(eye, tile)
            q[base + 2 * r, LANES : LANES + PAIR, :] = turned[:PAIR]
            q[base + 2 * r + 1, LANES : LANES + PAIR, :] = turned[PAIR:]

    if first:
        unpack(main_ref, rest_ref)
    else:

        @pl.when(t == 0)
        def _():
            unpack(old_main, old_rest)

        @pl.when(t > 0)
        def _():
            unpack(main_ref, rest_ref)

    for i in range(ROWS):
        ref, row = (lower_ref, i) if i < 2 else (upper_ref, i - 2)
        edge = jnp.clip(block * ROWS + i - 1, 0, edge_rows - 1)
        for k in range(2):
            uv[k, base + i, pl.ds(INNER, cols), :] = ref[k, row].astype(F32)
            uv[k, base + i, pl.ds(INNER - 1, 1), :] = edge_ref[2 * k, pl.ds(edge, 1), :]
            uv[k, base + i, pl.ds(INNER + cols, 1), :] = edge_ref[2 * k + 1, pl.ds(edge, 1), :]
    if first:

        @pl.when(t == 0)
        def _():
            for k in range(2):
                uv[k, base + 1, pl.ds(INNER, cols), :] = south_ref[k, 0].astype(F32)

    if last:

        @pl.when(t == pl.num_programs(0) - 1)
        def _():
            for k in range(2):
                uv[k, base + 2, pl.ds(INNER, cols), :] = north_ref[k, 0].astype(F32)

    def at(i):
        return base + i if i >= 0 else prior + ROWS + i

    step = 24
    for i in range(-1, ROWS - 1):
        for o in range(0, s.shape[1], step):
            s[at(i), pl.ds(o, step), :] = moved(
                q[at(i), pl.ds(o + 1, step), :],
                q[at(i), pl.ds(o + 2, step), :],
                q[at(i), pl.ds(o, step), :],
                q[at(i + 1), pl.ds(o + 1, step), :],
                q[at(i - 1), pl.ds(o + 1, step), :],
                uv[0, at(i), pl.ds(INNER - 1 + o, step), :],
                uv[1, at(i), pl.ds(INNER - 1 + o, step), :],
            )
    step = 32
    for i in range(-2, ROWS - 2):
        for o in range(0, cols, step):
            out_ref[i + 2, pl.ds(o, step), :] = moved(
                s[at(i), pl.ds(o + 1, step), :],
                s[at(i), pl.ds(o + 2, step), :],
                s[at(i), pl.ds(o, step), :],
                s[at(i + 1), pl.ds(o + 1, step), :],
                s[at(i - 1), pl.ds(o + 1, step), :],
                uv[0, at(i), pl.ds(INNER + o, step), :],
                uv[1, at(i), pl.ds(INNER + o, step), :],
            )


def transport(fields, index, starts, courant, halo, advected):
    field = fields[index]
    owners, length, _ = field.shape
    _, lat_rows, cols, levels = courant.shape
    edges, south, north = halo
    rows = length // 24
    blocks = rows // ROWS
    first = index == 0
    last = index == len(fields) - 1
    lead = 0 if first else 1
    offset = starts[index] // ROWS - lead
    wide = cols + 2 + (-cols - 2) % 24
    main = (owners, ROWS * 16, LANES)
    rest = (owners, ROWS * 8, LANES)
    pair = (2, 2, cols, LANES)
    pairs = lat_rows // 2

    def rest_at(count):
        return count * 2

    in_specs = [
        pl.BlockSpec(main, lambda t: (0, jnp.maximum(t - lead, 0), 0)),
        pl.BlockSpec(rest, lambda t: (0, rest_at(blocks) + jnp.maximum(t - lead, 0), 0)),
        pl.BlockSpec(pair, lambda t: (0, jnp.clip(2 * (t + offset) - 1, 0, pairs - 1), 0, 0)),
        pl.BlockSpec(pair, lambda t: (0, jnp.clip(2 * (t + offset), 0, pairs - 1), 0, 0)),
        pl.BlockSpec(edges.shape, lambda t: (0, 0, 0)),
        pl.BlockSpec(south.shape, lambda t: (0, 0, 0, 0)),
        pl.BlockSpec(north.shape, lambda t: (0, 0, 0, 0)),
    ]
    operands = [field, field, courant, courant, edges, south, north]
    aliases = {}
    if not first:
        old = fields[index - 1]
        old_blocks = old.shape[1] // 24 // ROWS
        in_specs += [
            pl.BlockSpec(main, lambda t: (0, old_blocks - 1, 0)),
            pl.BlockSpec(rest, lambda t: (0, rest_at(old_blocks) + old_blocks - 1, 0)),
            pl.BlockSpec(memory_space=pl.ANY),
        ]
        operands += [old, old, advected]
        aliases = {9: 0}
    return pl.pallas_call(
        functools.partial(transport_kernel, first, last, offset),
        grid=(blocks + lead,),
        in_specs=in_specs,
        out_specs=pl.BlockSpec(
            (ROWS, cols, levels), lambda t: (jnp.maximum(t, 1) - 1 + offset, 0, 0)
        ),
        out_shape=jax.ShapeDtypeStruct((lat_rows, cols, levels), F32),
        scratch_shapes=[
            pltpu.VMEM((2 * ROWS, LANES + PAIR, LANES), F32),
            pltpu.VMEM((2, 2 * ROWS, INNER + wide, LANES), F32),
            pltpu.VMEM((2 * ROWS, wide, LANES), F32),
        ],
        input_output_aliases=aliases,
        name="transport",
    )(*operands)


def packed_network(w_in, w_mid, w_out):
    inner, hidden = w_in.shape
    narrow = [w_out[i : i + inner] for i in range(0, hidden, inner)]
    return jnp.concatenate([w_in, w_mid, jnp.concatenate(narrow, axis=1)], axis=0)


def all_networks(own, owners):
    def from_device(array, x):
        return lax.ppermute(array, "lon", [(i ^ x, i) for i in range(owners)])

    even = jnp.stack([own] + [from_device(own, x) for x in range(2, owners, 2)])
    return jnp.concatenate([even, from_device(even, 1)], axis=0)


def network_kernel(blocks_ref, places_ref, state_ref, weight_ref, _, out_ref):
    def silu(v):
        return (v / (1.0 + jnp.exp(-v))).astype(BF16)

    levels = state_ref.shape[2]
    hidden = weight_ref.shape[2]
    x = state_ref[0].astype(BF16)
    one = silu(jnp.dot(x, weight_ref[0, :levels, :], preferred_element_type=F32))
    middle = weight_ref[0, levels : levels + hidden, :]
    two = silu(jnp.dot(one, middle, preferred_element_type=F32))
    tail = weight_ref[0, levels + hidden :, :]
    tail = jnp.concatenate([tail[:, i : i + levels] for i in range(0, hidden, levels)], axis=0)
    out_ref[0] = jnp.dot(two, tail, preferred_element_type=F32).astype(BF16)


def heat(advected, weights, blocks, places, empty):
    _, cols, levels = advected.shape
    across = cols // BC
    tile = (1, BC, levels)
    return pl.pallas_call(
        network_kernel,
        grid_spec=pltpu.PrefetchScalarGridSpec(
            num_scalar_prefetch=2,
            grid=(blocks.shape[0],),
            in_specs=[
                pl.BlockSpec(tile, lambda t, b, p: (b[t] // across, b[t] % across, 0)),
                pl.BlockSpec((1,) + weights.shape[1:], lambda t, b, p: (p[t], 0, 0)),
                pl.BlockSpec(memory_space=pl.ANY),
            ],
            out_specs=pl.BlockSpec(tile, lambda t, b, p: (b[t] // across, b[t] % across, 0)),
        ),
        out_shape=jax.ShapeDtypeStruct(empty.shape, BF16),
        input_output_aliases={4: 0},
        name="heat",
    )(blocks, places, advected, weights, empty)


def courant_halo(courant):
    bands = lax.axis_size("lat")
    owners = lax.axis_size("lon")
    up = [(i, i + 1) for i in range(bands - 1)]
    down = [(i + 1, i) for i in range(bands - 1)]
    south = lax.ppermute(courant[:, -1:], "lat", up)
    north = lax.ppermute(courant[:, :1], "lat", down)
    ahead = [(i, (i + 1) % owners) for i in range(owners)]
    back = [(j, i) for i, j in ahead]

    def column(at):
        parts = [part[:, :, at] for part in (south, courant, north)]
        return jnp.concatenate(parts, axis=1)

    west = lax.ppermute(column(-1), "lon", ahead)
    east = lax.ppermute(column(0), "lon", back)
    edges = jnp.stack([west, east], axis=1)
    return edges.reshape(4, edges.shape[2], edges.shape[3]).astype(F32), south, north


def chunk_sizes(rows):
    blocks = rows // ROWS
    cuts = [round(blocks * f) for f in (0.0, 0.3, 0.58, 0.82)] + [blocks]
    return [(b - a) * ROWS for a, b in zip(cuts, cuts[1:])]


def tiled_body(
    spectral,
    wavenumber_of_slot,
    filter_strength,
    courant,
    sunlit_blocks,
    sunlit_owner,
    radiation_in,
    radiation_mid,
    radiation_out,
):
    bands = lax.axis_size("lat")
    owners = lax.axis_size("lon")
    slots, parts, own_levels, degrees = spectral.shape
    _, lat_rows, lon_cols, levels = courant.shape
    latitudes = lat_rows * bands
    longitudes = lon_cols * owners
    own_waves = lax.dynamic_slice_in_dim(wavenumber_of_slot, lax.axis_index("lat") * slots, slots)
    degree = jnp.arange(degrees, dtype=jnp.int32)
    relative = (degree * (degree + 1)).astype(F32) / float(degrees * (degrees + 1))
    factor = 1.0 / (1.0 + filter_strength[:, None] * relative[None, :] * relative[None, :])

    place = lax.axis_index("lat").astype(jnp.int32).reshape(1)
    rows = lat_rows + 2 * EDGE
    sizes = chunk_sizes(rows)
    starts = [sum(sizes[:i]) for i in range(len(sizes))]
    lat_table = latitude_rows(degrees, latitudes, bands)
    grouped = regroup(spectral, own_waves, factor)
    received = []
    for start, size in zip(starts, sizes):
        piece = jnp.asarray(lat_table[:, start : start + size].reshape(bands * size, degrees))
        sent = latitude_transform(piece, grouped, place, bands)
        arrived = [
            lax.ppermute(sent[x], "lat", [(i, (i + x) % bands) for i in range(bands)])
            for x in range(1, bands)
        ]
        received.append([sent[0]] + arrived)

    lon_table = longitude_columns(wavenumber_of_slot, bands, longitudes, owners)
    halo = courant_halo(courant)
    own = packed_network(radiation_in[0], radiation_mid[0], radiation_out[0])
    weights = all_networks(own, owners)
    empty = jnp.zeros((lat_rows, lon_cols, levels), BF16)
    fields = []
    for pieces in received:
        sent = longitude_transform(pieces, lon_table, place)
        fields.append(lax.all_to_all(sent, "lon", split_axis=0, concat_axis=0, tiled=True))
    fields[0], empty, weights = lax.optimization_barrier((fields[0], empty, weights))

    advected = None
    for index in range(len(fields)):
        advected = transport(fields, index, starts, courant, halo, advected)

    blocks = sunlit_blocks.reshape(-1)
    other = sunlit_owner.reshape(-1) ^ lax.axis_index("lon").astype(jnp.int32)
    places = (other % 2) * (owners // 2) + other // 2
    return (advected, heat(advected, weights, blocks, places, empty))


def with_halo(array, sides, width):
    for axis, dim in sides:
        count, length = (lax.axis_size(axis), array.shape[dim])
        up = [(i, (i + 1) % count) for i in range(count)]
        down = [(j, i) for i, j in up]
        last = lax.slice_in_dim(array, length - width, length, axis=dim)
        leading = lax.slice_in_dim(array, 0, width, axis=dim)
        before = lax.ppermute(last, axis, up)
        after = lax.ppermute(leading, axis, down)
        array = jnp.concatenate([before, array, after], axis=dim)
    return array


def latitude_table(degrees, latitudes):
    degree_grid = lax.broadcasted_iota(jnp.int32, (degrees, latitudes), 0)
    row_index = lax.broadcasted_iota(jnp.int32, (degrees, latitudes), 1)
    phase_count = degree_grid * (2 * row_index + 1) % (4 * latitudes)
    phase_angle = phase_count.astype(jnp.float32) * (math.pi / (2.0 * latitudes))
    return (jnp.cos(phase_angle) * math.sqrt(2.0 / degrees)).astype(jnp.bfloat16)


def longitude_table(zonal_waves, longitudes):
    total_count = zonal_waves.shape[0]
    column_index = lax.broadcasted_iota(jnp.int32, (total_count, longitudes), 1)
    phase_count = zonal_waves[:, None] * column_index % longitudes
    phase_angle = phase_count.astype(jnp.float32) * (2.0 * math.pi / longitudes)
    scaling = 1.0 / math.sqrt(total_count)
    return jnp.stack(
        [jnp.cos(phase_angle) * scaling, -jnp.sin(phase_angle) * scaling], axis=1
    ).astype(jnp.bfloat16)


def damped(spectral, zonal_waves, strength, degrees):
    degree_grid = lax.broadcasted_iota(jnp.int32, spectral.shape, 3)
    component = lax.broadcasted_iota(jnp.int32, spectral.shape, 1)
    zonal_order = zonal_waves[:, None, None, None]
    retained = (degree_grid >= zonal_order) & ((component == 0) | (zonal_order > 0))
    relative = (degree_grid * (degree_grid + 1)).astype(jnp.float32) / float(
        degrees * (degrees + 1)
    )
    factor = 1.0 / (1.0 + strength[None, None, :, None] * relative * relative)
    return jnp.where(retained, spectral.astype(jnp.float32) * factor, 0.0).astype(jnp.bfloat16)


def plain_transport(padded, zonal, meridional):
    centre = padded[1:-1, 1:-1]
    northern = padded[2:, 1:-1]
    southern = padded[:-2, 1:-1]
    eastern = padded[1:-1, 2:]
    western = padded[1:-1, :-2]
    along = (
        centre
        - 0.5 * zonal * (eastern - western)
        + 0.5 * zonal * zonal * (eastern - 2.0 * centre + western)
    )
    return (
        along
        - 0.5 * meridional * (northern - southern)
        + 0.5 * meridional * meridional * (northern - 2.0 * centre + southern)
    )


def clear_poles(padded, depth, lat_dim):
    position = lax.axis_index("lat")
    extent = padded.shape[lat_dim]
    lat_index = lax.broadcasted_iota(jnp.int32, padded.shape, lat_dim)
    lower_rim = (position == 0) & (lat_index < depth)
    upper_rim = (position == lax.axis_size("lat") - 1) & (lat_index >= extent - depth)
    return jnp.where(lower_rim | upper_rim, jnp.zeros_like(padded), padded)


def regime_net(columns, w_in, w_mid, w_out):
    layer_one = jax.nn.silu(
        jnp.einsum("abcl,lh->abch", columns, w_in, preferred_element_type=jnp.float32)
    ).astype(jnp.bfloat16)
    layer_two = jax.nn.silu(
        jnp.einsum("abch,hg->abcg", layer_one, w_mid, preferred_element_type=jnp.float32)
    ).astype(jnp.bfloat16)
    return jnp.einsum("abcg,gl->abcl", layer_two, w_out, preferred_element_type=jnp.float32).astype(
        jnp.bfloat16
    )


def plain_body(
    spectral,
    wavenumber_of_slot,
    filter_strength,
    courant,
    sunlit_blocks,
    sunlit_owner,
    radiation_in,
    radiation_mid,
    radiation_out,
):
    own_count = spectral.shape[0]
    degrees = spectral.shape[3]
    own_waves = lax.dynamic_slice_in_dim(
        wavenumber_of_slot, lax.axis_index("lat") * own_count, own_count
    )
    filtered = damped(spectral, own_waves, filter_strength, degrees)
    coefficients = jnp.einsum(
        "scln,nj->sclj", filtered, latitude_table(degrees, courant.shape[1] * lax.axis_size("lat")), preferred_element_type=jnp.float32
    ).astype(jnp.bfloat16)
    wave_table = longitude_table(wavenumber_of_slot, courant.shape[2] * lax.axis_size("lon"))
    level_slab = jnp.einsum(
        "sclj,sck->jkl",
        lax.all_to_all(coefficients, "lat", split_axis=3, concat_axis=0, tiled=True),
        wave_table,
        preferred_element_type=jnp.float32,
    ).astype(jnp.bfloat16)
    grid_field = lax.all_to_all(level_slab, "lon", split_axis=1, concat_axis=2, tiled=True)
    zonal = courant[0].astype(jnp.float32)
    meridional = courant[1].astype(jnp.float32)
    stacked = jnp.concatenate([grid_field[None], courant], axis=0)
    widened = clear_poles(with_halo(stacked, (("lat", 1), ("lon", 2)), 2), 2, 1)
    tracer = widened[0].astype(jnp.float32)
    wide_zonal = widened[1].astype(jnp.float32)
    wide_meridional = widened[2].astype(jnp.float32)
    tracer = plain_transport(tracer, wide_zonal[1:-1, 1:-1], wide_meridional[1:-1, 1:-1])
    advected = plain_transport(tracer, zonal, meridional)
    state = advected.astype(jnp.bfloat16)
    lat_rows, lon_cols, levels = state.shape
    owners = lax.axis_size("lon")
    blocks = state.reshape(lat_rows * (lon_cols // BC), BC * levels)
    sunlit = sunlit_blocks.reshape(-1)
    destination = sunlit_owner.reshape(-1)
    listed = sunlit.shape[0]
    picked = jnp.take(blocks, sunlit, axis=0)
    position_of = destination * listed + lax.iota(jnp.int32, listed)
    select = (
        position_of[:, None] == lax.broadcasted_iota(jnp.int32, (listed, owners * listed), 1)
    ).astype(jnp.bfloat16)
    outgoing = jnp.einsum("sp,sd->pd", select, picked, preferred_element_type=jnp.float32).astype(
        jnp.bfloat16
    )
    outgoing = outgoing.reshape(owners, listed, BC, levels)
    computed = regime_net(
        lax.all_to_all(outgoing, "lon", split_axis=0, concat_axis=0, tiled=True),
        radiation_in[0],
        radiation_mid[0],
        radiation_out[0],
    )
    returned = lax.all_to_all(computed, "lon", split_axis=0, concat_axis=0, tiled=True).reshape(
        owners * listed, BC * levels
    )
    own_rows = jnp.einsum("sp,pd->sd", select, returned, preferred_element_type=jnp.float32).astype(
        jnp.bfloat16
    )
    covering = (
        sunlit[:, None] == lax.broadcasted_iota(jnp.int32, (listed, blocks.shape[0]), 1)
    ).astype(jnp.bfloat16)
    heating = jnp.einsum(
        "sb,sd->bd", covering, own_rows, preferred_element_type=jnp.float32
    ).astype(jnp.bfloat16)
    return (advected, heating.reshape(lat_rows, lon_cols, levels))


def longitudes_fit(count):
    return count % 4 == 0 and count * count < 1 << 23


def fits(spectral, courant, bands, owners):
    total, parts, levels, degrees = spectral.shape
    width = courant.shape[2] // owners
    height = courant.shape[1] // bands
    return (
        parts == 2
        and levels == LANES
        and levels // owners == 16
        and 2 * (total // bands) == MAIN + PAIR
        and degrees % LANES == 0
        and (total // bands) % 5 == 0
        and height % ROWS == 0
        and width % 32 == 0
        and owners & (owners - 1) == 0
        and longitudes_fit(courant.shape[2])
        and LANES < width + 2 * EDGE <= LANES + PAIR - 8
    )


def solution(mesh):
    in_specs = (
        P("lat", None, "lon", None),
        P(),
        P("lon"),
        P(None, "lat", "lon", None),
        P("lat", "lon", None),
        P("lat", "lon", None, None),
        P("lon", None, None),
        P("lon", None, None),
        P("lon", None, None),
    )
    out_specs = (P("lat", "lon", None), P("lat", "lon", None))
    bands, owners = mesh.shape["lat"], mesh.shape["lon"]

    def run(*arrays):
        body = tiled_body if fits(arrays[0], arrays[3], bands, owners) else plain_body
        return jax.shard_map(
            body, mesh=mesh, in_specs=in_specs, out_specs=out_specs, check_vma=False
        )(*arrays)

    return run
```
